512 devices in a mesh: dp: 8 (over z_hi, core), ctx: 64 (over x, z_lo, y).
Axes of the slice: x: 4, y: 4, z: 16 (z_hi: 4, z_lo: 4; z = z_hi * 4 + z_lo), core: 2. Of those that a mesh axis runs over, the one named last changes fastest.
Arguments:
- queries: bfloat16 [8, 2048, 8192], P('dp', None, 'ctx'), may hold values from -6 to 6
- keys: bfloat16 [8, 2048, 8192], P('dp', None, 'ctx'), may hold values from -6 to 6
- values: bfloat16 [8, 2048, 8192], P('dp', None, 'ctx'), may hold values from -6 to 6
- cotangent: bfloat16 [8, 2048, 8192], P('dp', None, 'ctx'), may hold values from -6 to 6
- residues: float32 [2048, 16], P(('dp', 'ctx')), may hold values from -1.5 to 1.5
- decays: float32 [2048, 16], P(('dp', 'ctx')), may hold values from 0.1 to 800
Outputs:
- mixed: bfloat16 [8, 2048, 8192], P('dp', None, 'ctx')
- grad_queries: bfloat16 [8, 2048, 8192], P('dp', None, 'ctx')
- grad_keys: bfloat16 [8, 2048, 8192], P('dp', None, 'ctx')
- grad_values: bfloat16 [8, 2048, 8192], P('dp', None, 'ctx')
- grad_residues: float32 [2048, 16], P(('dp', 'ctx'))
The draws below stay inside these ranges and needn't reach their ends.
All inputs are finite; a program needn't handle non-finite values.
Results may differ from the reference program's by a relative error of at most 0.0057.
Values may be sent and summed in bfloat16 or wider, within the bound.
A program may use at most 64 MiB of HBM per device.

```python
import math
import jax
import jax.numpy as jnp
from jax import lax

D = 2048
ORDER = 16
SEQS = 8
LENGTH = 8192


def level_of(own_key, extent, shards, smallest, high):
    gain, own = 1.0, jax.random.fold_in(own_key, 6)
    for axis_at, blocks in shards:
        heights = jnp.exp(jax.random.uniform(jax.random.fold_in(own, axis_at), (blocks,), jnp.float32, smallest / len(shards), high / len(shards)))
        gain = gain * jnp.repeat(heights, extent[axis_at] // blocks).reshape([-1 if axis == axis_at else 1 for axis in range(len(extent))])
    return gain


def normal_values(key, shape, spread, reach, cuts=(), kind=jnp.bfloat16):
    result = jax.random.normal(key, shape, jnp.float32) * spread
    if len(cuts) > 0:
        result = level_of(key, shape, cuts, -0.22, 0.18) * result
    return jnp.clip(result, min=-reach, max=reach).astype(kind)


def setup_inputs(seed: int = 0) -> dict:
    streams_of = jax.random.split(jax.random.key(seed), 7)
    return {
        "queries": normal_values(streams_of[0], (SEQS, D, LENGTH), 1.0, 6.0, ((0, 8), (2, 64))),
        "keys": normal_values(streams_of[1], (SEQS, D, LENGTH), 1.0, 6.0, ((0, 8), (2, 64))),
        "values": normal_values(streams_of[2], (SEQS, D, LENGTH), 1.0, 6.0, ((0, 8), (2, 64))),
        "cotangent": normal_values(streams_of[3], (SEQS, D, LENGTH), 1.0, 6.0, ((0, 8), (2, 64))),
        "residues": normal_values(streams_of[4], (D, ORDER), 0.25, 1.5, ((0, 512),), jnp.float32),
        "decays": jnp.clip(jnp.exp(math.log(800.0) - 8.987197 * jax.random.uniform(streams_of[5], (D, ORDER), jnp.float32) ** level_of(streams_of[5], (D, ORDER), ((0, 512),), -0.2, 0.2)), 0.1, 800.0),
    }


def reference(queries, keys, values, cotangent, residues, decays):
    seq_count, channels, length = keys.shape
    padded = 2 * length
    steps_t = jnp.arange(length, dtype=jnp.float32) / length
    mode_scale = jnp.sqrt(1.0 - jnp.exp(-2.0 * decays / length))
    weighted = residues * mode_scale
    filter_taps = jnp.zeros((channels, length), jnp.float32)
    for mode_idx in range(ORDER):
        filter_taps = filter_taps + weighted[:, mode_idx:mode_idx + 1] * jnp.exp(-decays[:, mode_idx:mode_idx + 1] * steps_t[None, :])
    filt_spec = jnp.fft.rfft(filter_taps, n=padded, axis=-1)
    gated_in = (keys.astype(jnp.float32) * values.astype(jnp.float32)).astype(jnp.bfloat16)
    gated_grad = (cotangent.astype(jnp.float32) * queries.astype(jnp.float32)).astype(jnp.bfloat16)

    def one_sequence(running, pair_in):
        signal, grad_signal = pair_in
        spectrum = jnp.fft.rfft(signal.astype(jnp.float32), n=padded, axis=-1)
        grad_spec = jnp.fft.rfft(grad_signal.astype(jnp.float32), n=padded, axis=-1)
        convolved = jnp.fft.irfft(spectrum * filt_spec, n=padded, axis=-1)[:, :length].astype(jnp.bfloat16)
        back_conv = jnp.fft.irfft(jnp.conj(filt_spec) * grad_spec, n=padded, axis=-1)[:, :length].astype(jnp.bfloat16)
        running = running + jnp.fft.irfft(jnp.conj(spectrum) * grad_spec, n=padded, axis=-1)[:, :length]
        return (running, (convolved, back_conv))
    grad_taps, (convolved, back_conv) = lax.scan(one_sequence, jnp.zeros((channels, length), jnp.float32), (gated_in, gated_grad))
    conv_f = convolved.astype(jnp.float32)
    back_f = back_conv.astype(jnp.float32)
    mixed = (queries.astype(jnp.float32) * conv_f).astype(jnp.bfloat16)
    grad_queries = (cotangent.astype(jnp.float32) * conv_f).astype(jnp.bfloat16)
    grad_keys = (back_f * values.astype(jnp.float32)).astype(jnp.bfloat16)
    grad_values = (back_f * keys.astype(jnp.float32)).astype(jnp.bfloat16)
    columns = []
    for mode_idx in range(ORDER):
        columns.append(lax.optimization_barrier(jnp.sum(grad_taps * jnp.exp(-decays[:, mode_idx:mode_idx + 1] * steps_t[None, :]), axis=1)))
    grad_residues = jnp.stack(columns, axis=1) * mode_scale / math.sqrt(seq_count * length)
    return (mixed, grad_queries, grad_keys, grad_values, grad_residues)
```

```python
import math

import jax
import jax.numpy as jnp
from jax import lax
from jax.sharding import PartitionSpec as P

exact_mode = lax.Precision.HIGHEST


def shift_along(x, axis, n, step):
    if step > 0:
        pairs = [(i, i + step) for i in range(n - step)]
    else:
        pairs = [(i, i + step) for i in range(-step, n)]
    return lax.ppermute(x, axis, perm=pairs)


def chunk_scan(state, chunk_decay, axis, n, direction):
    carry = shift_along(state, axis, n, direction)
    hop = 1
    while hop < n:
        carry = carry + jnp.exp(-chunk_decay * hop) * shift_along(carry, axis, n, direction * hop)
        hop *= 2
    return carry


def body(queries, keys, values, cotangent, residues, decays):
    n_dp = lax.axis_size("dp")
    n_ctx = lax.axis_size("ctx")
    seq_count, channels, chunk = keys.shape
    order = residues.shape[1]
    length = chunk * n_ctx
    f32 = jnp.float32

    params = lax.all_gather(
        jnp.concatenate([residues, decays], axis=1), ("dp", "ctx"), axis=0, tiled=True
    )
    dec = params[:, order:]
    scale = jnp.sqrt(1.0 - jnp.exp(-2.0 * dec / length))
    weight = params[:, :order] * scale

    gated_in = (keys.astype(f32) * values.astype(f32)).astype(jnp.bfloat16)
    gated_grad = (cotangent.astype(f32) * queries.astype(f32)).astype(jnp.bfloat16)
    g = gated_in[0].astype(f32)
    gg = gated_grad[0].astype(f32)

    pos = jnp.arange(chunk, dtype=f32)
    mid = chunk // 2
    dk = dec[:, :, None]
    grow = jnp.exp(dk * ((pos - mid) / length))
    shrink = jnp.exp(-dk * ((pos - mid) / length))
    upper = (pos[:, None] <= pos[None, :]).astype(f32)
    lower = (pos[:, None] >= pos[None, :]).astype(f32)

    end_fwd = jnp.sum(g[:, None, :] * jnp.exp(-dk * ((chunk - 1 - pos) / length)), axis=-1)
    start_bwd = jnp.sum(gg[:, None, :] * jnp.exp(-dk * (pos / length)), axis=-1)
    chunk_decay = dec * (chunk / length)
    carry_fwd = chunk_scan(end_fwd, chunk_decay, "ctx", n_ctx, 1)
    carry_bwd = chunk_scan(start_bwd, chunk_decay, "ctx", n_ctx, -1)

    fwd_state = shrink * jnp.einsum(
        "dnc,ct->dnt", g[:, None, :] * grow, upper, precision=exact_mode
    )
    bwd_state = grow * jnp.einsum(
        "dnc,ct->dnt", gg[:, None, :] * shrink, lower, precision=exact_mode
    )
    conv_intra = jnp.sum(weight[:, :, None] * fwd_state, axis=1)
    back_intra = jnp.sum(weight[:, :, None] * bwd_state, axis=1)
    cross_intra = jnp.sum(gg[:, None, :] * fwd_state, axis=-1)

    lead_fwd = jnp.exp(-dk * ((pos + 1) / length))
    lead_bwd = jnp.exp(-dk * ((chunk - pos) / length))
    conv_full = conv_intra + jnp.sum((weight * carry_fwd)[:, :, None] * lead_fwd, axis=1)
    back_full = back_intra + jnp.sum((weight * carry_bwd)[:, :, None] * lead_bwd, axis=1)
    cross = cross_intra + carry_fwd * jnp.sum(gg[:, None, :] * lead_fwd, axis=-1)

    total = lax.psum_scatter(cross, ("dp", "ctx"), scatter_dimension=0, tiled=True)
    own_scale = jnp.sqrt(1.0 - jnp.exp(-2.0 * decays / length))
    grad_residues = total * own_scale / math.sqrt(seq_count * n_dp * length)

    conv_f = conv_full.astype(jnp.bfloat16).astype(f32)[None]
    back_f = back_full.astype(jnp.bfloat16).astype(f32)[None]
    mixed = (queries.astype(f32) * conv_f).astype(jnp.bfloat16)
    grad_queries = (cotangent.astype(f32) * conv_f).astype(jnp.bfloat16)
    grad_keys = (back_f * values.astype(f32)).astype(jnp.bfloat16)
    grad_values = (back_f * keys.astype(f32)).astype(jnp.bfloat16)
    return (mixed, grad_queries, grad_keys, grad_values, grad_residues)


def solution(mesh):
    return jax.shard_map(
        body,
        mesh=mesh,
        in_specs=(
            P("dp", None, "ctx"),
            P("dp", None, "ctx"),
            P("dp", None, "ctx"),
            P("dp", None, "ctx"),
            P(("dp", "ctx"), None),
            P(("dp", "ctx"), None),
        ),
        out_specs=(
            P("dp", None, "ctx"),
            P("dp", None, "ctx"),
            P("dp", None, "ctx"),
            P("dp", None, "ctx"),
            P(("dp", "ctx"), None),
        ),
        check_vma=False,
    )
```

```python
import math

import jax
import jax.numpy as jnp
from jax import lax
from jax.sharding import PartitionSpec as P

exact_mode = lax.Precision.HIGHEST


def body(queries, keys, values, cotangent, residues, decays):
    n_dp = lax.axis_size("dp")
    n_ctx = lax.axis_size("ctx")
    ctx_at = lax.axis_index("ctx")
    seq_count, channels, chunk = keys.shape
    block, order = residues.shape
    length = chunk * n_ctx
    f32 = jnp.float32

    own = jnp.concatenate([residues, decays], axis=1)
    part = lax.all_to_all(
        jnp.broadcast_to(own[None], (n_ctx,) + own.shape), "ctx", 0, 0, tiled=True
    )
    params = lax.all_to_all(
        jnp.broadcast_to(part[None], (n_dp,) + part.shape), "dp", 0, 0, tiled=True
    ).reshape(channels, 2 * order)
    dec = params[:, order:]
    scale = jnp.sqrt(1.0 - jnp.exp(-2.0 * dec / length))
    weight = params[:, :order] * scale

    gated_in = (keys.astype(f32) * values.astype(f32)).astype(jnp.bfloat16)
    gated_grad = (cotangent.astype(f32) * queries.astype(f32)).astype(jnp.bfloat16)
    g = gated_in[0].astype(f32)
    gg = gated_grad[0].astype(f32)

    pos = jnp.arange(chunk, dtype=f32)
    mid = chunk // 2
    dk = dec[:, :, None]
    grow = jnp.exp(dk * ((pos - mid) / length))
    shrink = jnp.exp(-dk * ((pos - mid) / length))
    upper = (pos[:, None] <= pos[None, :]).astype(f32)
    lower = (pos[:, None] >= pos[None, :]).astype(f32)

    fwd_state = shrink * jnp.einsum(
        "dnc,ct->dnt", g[:, None, :] * grow, upper, precision=exact_mode
    )
    bwd_state = grow * jnp.einsum(
        "dnc,ct->dnt", gg[:, None, :] * shrink, lower, precision=exact_mode
    )
    conv_intra = jnp.sum(weight[:, :, None] * fwd_state, axis=1)
    back_intra = jnp.sum(weight[:, :, None] * bwd_state, axis=1)
    cross_intra = jnp.sum(gg[:, None, :] * fwd_state, axis=-1)
    lead_fwd = jnp.exp(-dk * ((pos + 1) / length))
    lead_bwd = jnp.exp(-dk * ((chunk - pos) / length))
    cross_lead = jnp.sum(gg[:, None, :] * lead_fwd, axis=-1)
    end_fwd = fwd_state[:, :, chunk - 1]
    start_bwd = bwd_state[:, :, 0]

    groups = channels // (n_dp * n_ctx)
    stats = jnp.concatenate([end_fwd, start_bwd, cross_intra, cross_lead], axis=1)
    stats = stats.reshape(n_dp, n_ctx, groups, 4 * order)
    stats = lax.all_to_all(stats, "ctx", 1, 1, tiled=True)
    s_fwd = stats[..., :order]
    s_bwd = stats[..., order : 2 * order]
    c_intra = stats[..., 2 * order : 3 * order]
    c_lead = stats[..., 3 * order :]
    dec_grp = lax.dynamic_slice_in_dim(
        dec.reshape(n_dp, n_ctx, groups, order), ctx_at, 1, axis=1
    )
    here = jnp.arange(n_ctx)
    gap = (here[:, None] - here[None, :]).astype(f32)
    decay_dims = dec_grp[:, :, None, :, :]
    ahead = jnp.where(
        (gap > 0)[None, :, :, None, None],
        jnp.exp(-decay_dims * ((gap - 1.0) * (chunk / length))[None, :, :, None, None]),
        0.0,
    )
    behind = jnp.where(
        (gap < 0)[None, :, :, None, None],
        jnp.exp(-decay_dims * ((-gap - 1.0) * (chunk / length))[None, :, :, None, None]),
        0.0,
    )
    carry_fwd = jnp.sum(ahead * s_fwd[:, None], axis=2)
    carry_bwd = jnp.sum(behind * s_bwd[:, None], axis=2)
    cross_grp = jnp.sum(c_intra + carry_fwd * c_lead, axis=1)
    carries = lax.all_to_all(
        jnp.concatenate([carry_fwd, carry_bwd], axis=-1), "ctx", 1, 1, tiled=True
    ).reshape(channels, 2 * order)
    carry_fwd = carries[:, :order]
    carry_bwd = carries[:, order:]
    total = jnp.sum(lax.all_to_all(cross_grp, "dp", 0, 0, tiled=True), axis=0)

    own_scale = jnp.sqrt(1.0 - jnp.exp(-2.0 * decays / length))
    grad_residues = total * own_scale / math.sqrt(seq_count * n_dp * length)

    conv_full = conv_intra + jnp.sum((weight * carry_fwd)[:, :, None] * lead_fwd, axis=1)
    back_full = back_intra + jnp.sum((weight * carry_bwd)[:, :, None] * lead_bwd, axis=1)
    conv_f = conv_full.astype(jnp.bfloat16).astype(f32)[None]
    back_f = back_full.astype(jnp.bfloat16).astype(f32)[None]
    mixed = (queries.astype(f32) * conv_f).astype(jnp.bfloat16)
    grad_queries = (cotangent.astype(f32) * conv_f).astype(jnp.bfloat16)
    grad_keys = (back_f * values.astype(f32)).astype(jnp.bfloat16)
    grad_values = (back_f * keys.astype(f32)).astype(jnp.bfloat16)
    return (mixed, grad_queries, grad_keys, grad_values, grad_residues)


def solution(mesh):
    return jax.shard_map(
        body,
        mesh=mesh,
        in_specs=(
            P("dp", None, "ctx"),
            P("dp", None, "ctx"),
            P("dp", None, "ctx"),
            P("dp", None, "ctx"),
            P(("dp", "ctx"), None),
            P(("dp", "ctx"), None),
        ),
        out_specs=(
            P("dp", None, "ctx"),
            P("dp", None, "ctx"),
            P("dp", None, "ctx"),
            P("dp", None, "ctx"),
            P(("dp", "ctx"), None),
        ),
        check_vma=False,
    )
```

```python
import math

import jax
import jax.numpy as jnp
from jax import lax
from jax.sharding import PartitionSpec as P

exact_mode = lax.Precision.HIGHEST


def body(queries, keys, values, cotangent, residues, decays):
    n_dp = lax.axis_size("dp")
    n_ctx = lax.axis_size("ctx")
    ctx_at = lax.axis_index("ctx")
    seq_count, channels, chunk = keys.shape
    block, order = residues.shape
    length = chunk * n_ctx
    f32 = jnp.float32

    own = jnp.concatenate([residues, decays], axis=1)
    part = lax.all_to_all(
        jnp.broadcast_to(own[None], (n_dp,) + own.shape), "dp", 0, 0, tiled=True
    ).reshape(n_dp, 1, block, 2 * order)
    params = lax.all_to_all(
        jnp.broadcast_to(part, (n_dp, n_ctx, block, 2 * order)), "ctx", 1, 1, tiled=True
    ).reshape(channels, 2 * order)
    dec = params[:, order:]
    scale = jnp.sqrt(1.0 - jnp.exp(-2.0 * dec / length))
    weight = params[:, :order] * scale

    gated_in = (keys.astype(f32) * values.astype(f32)).astype(jnp.bfloat16)
    gated_grad = (cotangent.astype(f32) * queries.astype(f32)).astype(jnp.bfloat16)
    g = gated_in[0].astype(f32)
    gg = gated_grad[0].astype(f32)

    pos = jnp.arange(chunk, dtype=f32)
    mid = chunk // 2
    dk = dec[:, :, None]
    grow = jnp.exp(dk * ((pos - mid) / length))
    shrink = jnp.exp(-dk * ((pos - mid) / length))
    upper = (pos[:, None] <= pos[None, :]).astype(f32)
    lower = (pos[:, None] >= pos[None, :]).astype(f32)

    fwd_state = shrink * jnp.einsum(
        "dnc,ct->dnt", g[:, None, :] * grow, upper, precision=exact_mode
    )
    bwd_state = grow * jnp.einsum(
        "dnc,ct->dnt", gg[:, None, :] * shrink, lower, precision=exact_mode
    )
    conv_intra = jnp.sum(weight[:, :, None] * fwd_state, axis=1)
    back_intra = jnp.sum(weight[:, :, None] * bwd_state, axis=1)
    cross_intra = jnp.sum(gg[:, None, :] * fwd_state, axis=-1)
    lead_fwd = shrink * jnp.exp(-dk * ((mid + 1) / length))
    lead_bwd = grow * jnp.exp(-dk * ((chunk - mid) / length))
    cross_lead = jnp.sum(gg[:, None, :] * lead_fwd, axis=-1)
    end_fwd = fwd_state[:, :, chunk - 1]
    start_bwd = bwd_state[:, :, 0]

    groups = channels // (n_dp * n_ctx)
    stats = jnp.concatenate([end_fwd, start_bwd, cross_intra, cross_lead], axis=1)
    stats = stats.reshape(n_dp, n_ctx, groups, 4 * order)
    stats = lax.all_to_all(stats, "ctx", 1, 1, tiled=True)
    s_fwd = stats[..., :order]
    s_bwd = stats[..., order : 2 * order]
    c_intra = stats[..., 2 * order : 3 * order]
    c_lead = stats[..., 3 * order :]
    dec_grp = lax.dynamic_slice_in_dim(
        dec.reshape(n_dp, n_ctx, groups, order), ctx_at, 1, axis=1
    )
    hop_decay = dec_grp * (chunk / length)

    def exclusive_scan(state, sign):
        pad = jnp.zeros_like(state[:, :1])
        if sign > 0:
            carry = jnp.concatenate([pad, state[:, :-1]], axis=1)
        else:
            carry = jnp.concatenate([state[:, 1:], pad], axis=1)
        hop = 1
        while hop < n_ctx:
            fill = jnp.zeros_like(carry[:, :hop])
            if sign > 0:
                moved = jnp.concatenate([fill, carry[:, :-hop]], axis=1)
            else:
                moved = jnp.concatenate([carry[:, hop:], fill], axis=1)
            carry = carry + jnp.exp(-hop_decay * hop) * moved
            hop *= 2
        return carry

    carry_fwd = exclusive_scan(s_fwd, 1)
    carry_bwd = exclusive_scan(s_bwd, -1)
    cross_grp = jnp.sum(c_intra + carry_fwd * c_lead, axis=1)
    carries = lax.all_to_all(
        jnp.concatenate([carry_fwd, carry_bwd], axis=-1), "ctx", 1, 1, tiled=True
    ).reshape(channels, 2 * order)
    carry_fwd = carries[:, :order]
    carry_bwd = carries[:, order:]
    total = jnp.sum(lax.all_to_all(cross_grp, "dp", 0, 0, tiled=True), axis=0)

    own_scale = jnp.sqrt(1.0 - jnp.exp(-2.0 * decays / length))
    grad_residues = total * own_scale / math.sqrt(seq_count * n_dp * length)

    conv_full = conv_intra + jnp.sum((weight * carry_fwd)[:, :, None] * lead_fwd, axis=1)
    back_full = back_intra + jnp.sum((weight * carry_bwd)[:, :, None] * lead_bwd, axis=1)
    conv_f = conv_full.astype(jnp.bfloat16).astype(f32)[None]
    back_f = back_full.astype(jnp.bfloat16).astype(f32)[None]
    mixed = (queries.astype(f32) * conv_f).astype(jnp.bfloat16)
    grad_queries = (cotangent.astype(f32) * conv_f).astype(jnp.bfloat16)
    grad_keys = (back_f * values.astype(f32)).astype(jnp.bfloat16)
    grad_values = (back_f * keys.astype(f32)).astype(jnp.bfloat16)
    return (mixed, grad_queries, grad_keys, grad_values, grad_residues)


def solution(mesh):
    return jax.shard_map(
        body,
        mesh=mesh,
        in_specs=(
            P("dp", None, "ctx"),
            P("dp", None, "ctx"),
            P("dp", None, "ctx"),
            P("dp", None, "ctx"),
            P(("dp", "ctx"), None),
            P(("dp", "ctx"), None),
        ),
        out_specs=(
            P("dp", None, "ctx"),
            P("dp", None, "ctx"),
            P("dp", None, "ctx"),
            P("dp", None, "ctx"),
            P(("dp", "ctx"), None),
        ),
        check_vma=False,
    )
```

```python
import functools
import math

import jax
import jax.numpy as jnp
from jax import lax
from jax.experimental import pallas as pl
from jax.sharding import PartitionSpec as P

exact_mode = lax.Precision.HIGHEST


def split_dot(x, tri):
    hi = x.astype(jnp.bfloat16)
    lo = (x - hi.astype(jnp.float32)).astype(jnp.bfloat16)
    return jnp.dot(hi, tri, preferred_element_type=jnp.float32) + jnp.dot(
        lo, tri, preferred_element_type=jnp.float32
    )


def chunk_kernel(k_ref, v_ref, c_ref, q_ref, dec_ref, w_ref, conv_ref, back_ref, stats_ref, *, length):
    f32 = jnp.float32
    rows, chunk = k_ref.shape
    order = dec_ref.shape[1]
    mid = chunk // 2
    g = (k_ref[...].astype(f32) * v_ref[...].astype(f32)).astype(jnp.bfloat16).astype(f32)
    gg = (c_ref[...].astype(f32) * q_ref[...].astype(f32)).astype(jnp.bfloat16).astype(f32)
    dec = dec_ref[...]
    w = w_ref[...]
    pos = lax.broadcasted_iota(jnp.int32, (1, chunk), 1).astype(f32)
    row_at = lax.broadcasted_iota(jnp.int32, (chunk, chunk), 0)
    col_at = lax.broadcasted_iota(jnp.int32, (chunk, chunk), 1)
    upper = (row_at <= col_at).astype(jnp.bfloat16)
    lower = (row_at >= col_at).astype(jnp.bfloat16)
    offset = (pos - mid) / length
    conv = jnp.zeros((rows, chunk), f32)
    back = jnp.zeros((rows, chunk), f32)
    for n in range(order):
        a = dec[:, n : n + 1]
        grow = jnp.exp(a * offset)
        shrink = jnp.exp(-a * offset)
        fwd = shrink * split_dot(g * grow, upper)
        bwd = grow * split_dot(gg * shrink, lower)
        conv = conv + w[:, n : n + 1] * fwd
        back = back + w[:, n : n + 1] * bwd
        stats_ref[:, n : n + 1] = fwd[:, chunk - 1 :]
        stats_ref[:, order + n : order + n + 1] = bwd[:, :1]
        stats_ref[:, 2 * order + n : 2 * order + n + 1] = jnp.sum(gg * fwd, axis=1, keepdims=True)
        stats_ref[:, 3 * order + n : 3 * order + n + 1] = jnp.sum(
            gg * shrink, axis=1, keepdims=True
        ) * jnp.exp(-a * ((mid + 1) / length))
    conv_ref[...] = conv
    back_ref[...] = back


def chunk_pass(keys, values, cotangent, queries, dec, weight, length, rows=256):
    channels, chunk = keys.shape
    order = dec.shape[1]
    rows = min(rows, channels)
    wide = pl.BlockSpec((rows, chunk), lambda i: (i, 0))
    narrow = pl.BlockSpec((rows, order), lambda i: (i, 0))
    return pl.pallas_call(
        functools.partial(chunk_kernel, length=length),
        grid=(channels // rows,),
        in_specs=[wide, wide, wide, wide, narrow, narrow],
        out_specs=[wide, wide, pl.BlockSpec((rows, 4 * order), lambda i: (i, 0))],
        out_shape=[
            jax.ShapeDtypeStruct((channels, chunk), jnp.float32),
            jax.ShapeDtypeStruct((channels, chunk), jnp.float32),
            jax.ShapeDtypeStruct((channels, 4 * order), jnp.float32),
        ],
    )(keys, values, cotangent, queries, dec, weight)


def body(queries, keys, values, cotangent, residues, decays):
    n_dp = lax.axis_size("dp")
    n_ctx = lax.axis_size("ctx")
    ctx_at = lax.axis_index("ctx")
    seq_count, channels, chunk = keys.shape
    block, order = residues.shape
    length = chunk * n_ctx
    f32 = jnp.float32

    own = jnp.concatenate([residues, decays], axis=1)
    part = lax.all_to_all(
        jnp.broadcast_to(own[None], (n_dp,) + own.shape), "dp", 0, 0, tiled=True
    ).reshape(n_dp, 1, block, 2 * order)
    params = lax.all_to_all(
        jnp.broadcast_to(part, (n_dp, n_ctx, block, 2 * order)), "ctx", 1, 1, tiled=True
    ).reshape(channels, 2 * order)
    dec = params[:, order:]
    scale = jnp.sqrt(1.0 - jnp.exp(-2.0 * dec / length))
    weight = params[:, :order] * scale

    pos = jnp.arange(chunk, dtype=f32)
    dk = dec[:, :, None]
    conv_intra, back_intra, stats = chunk_pass(
        keys[0], values[0], cotangent[0], queries[0], dec, weight, length
    )
    lead_fwd = jnp.exp(-dk * ((pos + 1) / length))
    lead_bwd = jnp.exp(-dk * ((chunk - pos) / length))

    groups = channels // (n_dp * n_ctx)
    stats = stats.reshape(n_dp, n_ctx, groups, 4 * order)
    stats = lax.all_to_all(stats, "ctx", 1, 1, tiled=True)
    s_fwd = stats[..., :order]
    s_bwd = stats[..., order : 2 * order]
    c_intra = stats[..., 2 * order : 3 * order]
    c_lead = stats[..., 3 * order :]
    dec_grp = lax.dynamic_slice_in_dim(
        dec.reshape(n_dp, n_ctx, groups, order), ctx_at, 1, axis=1
    )
    hop_decay = dec_grp * (chunk / length)

    def exclusive_scan(state, sign):
        pad = jnp.zeros_like(state[:, :1])
        if sign > 0:
            carry = jnp.concatenate([pad, state[:, :-1]], axis=1)
        else:
            carry = jnp.concatenate([state[:, 1:], pad], axis=1)
        hop = 1
        while hop < n_ctx:
            fill = jnp.zeros_like(carry[:, :hop])
            if sign > 0:
                moved = jnp.concatenate([fill, carry[:, :-hop]], axis=1)
            else:
                moved = jnp.concatenate([carry[:, hop:], fill], axis=1)
            carry = carry + jnp.exp(-hop_decay * hop) * moved
            hop *= 2
        return carry

    carry_fwd = exclusive_scan(s_fwd, 1)
    carry_bwd = exclusive_scan(s_bwd, -1)
    cross_grp = jnp.sum(c_intra + carry_fwd * c_lead, axis=1)
    carries = lax.all_to_all(
        jnp.concatenate([carry_fwd, carry_bwd], axis=-1), "ctx", 1, 1, tiled=True
    ).reshape(channels, 2 * order)
    carry_fwd = carries[:, :order]
    carry_bwd = carries[:, order:]
    total = jnp.sum(lax.all_to_all(cross_grp, "dp", 0, 0, tiled=True), axis=0)

    own_scale = jnp.sqrt(1.0 - jnp.exp(-2.0 * decays / length))
    grad_residues = total * own_scale / math.sqrt(seq_count * n_dp * length)

    conv_full = conv_intra + jnp.sum((weight * carry_fwd)[:, :, None] * lead_fwd, axis=1)
    back_full = back_intra + jnp.sum((weight * carry_bwd)[:, :, None] * lead_bwd, axis=1)
    conv_f = conv_full.astype(jnp.bfloat16).astype(f32)[None]
    back_f = back_full.astype(jnp.bfloat16).astype(f32)[None]
    mixed = (queries.astype(f32) * conv_f).astype(jnp.bfloat16)
    grad_queries = (cotangent.astype(f32) * conv_f).astype(jnp.bfloat16)
    grad_keys = (back_f * values.astype(f32)).astype(jnp.bfloat16)
    grad_values = (back_f * keys.astype(f32)).astype(jnp.bfloat16)
    return (mixed, grad_queries, grad_keys, grad_values, grad_residues)


def solution(mesh):
    return jax.shard_map(
        body,
        mesh=mesh,
        in_specs=(
            P("dp", None, "ctx"),
            P("dp", None, "ctx"),
            P("dp", None, "ctx"),
            P("dp", None, "ctx"),
            P(("dp", "ctx"), None),
            P(("dp", "ctx"), None),
        ),
        out_specs=(
            P("dp", None, "ctx"),
            P("dp", None, "ctx"),
            P("dp", None, "ctx"),
            P("dp", None, "ctx"),
            P(("dp", "ctx"), None),
        ),
        check_vma=False,
    )
```

```python
import functools
import math

import jax
import jax.numpy as jnp
from jax import lax
from jax.experimental import pallas as pl
from jax.sharding import PartitionSpec as P

exact_mode = lax.Precision.HIGHEST


def split_dot(x, tri):
    hi = x.astype(jnp.bfloat16)
    lo = (x - hi.astype(jnp.float32)).astype(jnp.bfloat16)
    return jnp.dot(hi, tri, preferred_element_type=jnp.float32) + jnp.dot(
        lo, tri, preferred_element_type=jnp.float32
    )


def chunk_kernel(k_ref, v_ref, c_ref, q_ref, dec_ref, w_ref, conv_ref, back_ref, stats_ref, *, length):
    f32 = jnp.float32
    rows, chunk = k_ref.shape
    order = dec_ref.shape[1]
    mid = chunk // 2
    g = (k_ref[...].astype(f32) * v_ref[...].astype(f32)).astype(jnp.bfloat16).astype(f32)
    gg = (c_ref[...].astype(f32) * q_ref[...].astype(f32)).astype(jnp.bfloat16).astype(f32)
    dec = dec_ref[...]
    w = w_ref[...]
    pos = lax.broadcasted_iota(jnp.int32, (1, chunk), 1).astype(f32)
    row_at = lax.broadcasted_iota(jnp.int32, (chunk, chunk), 0)
    col_at = lax.broadcasted_iota(jnp.int32, (chunk, chunk), 1)
    upper = (row_at <= col_at).astype(jnp.bfloat16)
    lower = (row_at >= col_at).astype(jnp.bfloat16)
    offset = (pos - mid) / length
    conv = jnp.zeros((rows, chunk), f32)
    back = jnp.zeros((rows, chunk), f32)
    for n in range(order):
        a = dec[:, n : n + 1]
        grow = jnp.exp(a * offset)
        shrink = jnp.exp(-a * offset)
        fwd = shrink * split_dot(g * grow, upper)
        bwd = grow * split_dot(gg * shrink, lower)
        conv = conv + w[:, n : n + 1] * fwd
        back = back + w[:, n : n + 1] * bwd
        stats_ref[:, n : n + 1] = fwd[:, chunk - 1 :]
        stats_ref[:, order + n : order + n + 1] = bwd[:, :1]
        stats_ref[:, 2 * order + n : 2 * order + n + 1] = jnp.sum(gg * fwd, axis=1, keepdims=True)
        stats_ref[:, 3 * order + n : 3 * order + n + 1] = jnp.sum(
            gg * shrink, axis=1, keepdims=True
        ) * jnp.exp(-a * ((mid + 1) / length))
    conv_ref[...] = conv
    back_ref[...] = back


def chunk_pass(keys, values, cotangent, queries, dec, weight, length, rows=256):
    channels, chunk = keys.shape
    order = dec.shape[1]
    rows = min(rows, channels)
    wide = pl.BlockSpec((rows, chunk), lambda i: (i, 0))
    narrow = pl.BlockSpec((rows, order), lambda i: (i, 0))
    return pl.pallas_call(
        functools.partial(chunk_kernel, length=length),
        grid=(channels // rows,),
        in_specs=[wide, wide, wide, wide, narrow, narrow],
        out_specs=[wide, wide, pl.BlockSpec((rows, 4 * order), lambda i: (i, 0))],
        out_shape=[
            jax.ShapeDtypeStruct((channels, chunk), jnp.float32),
            jax.ShapeDtypeStruct((channels, chunk), jnp.float32),
            jax.ShapeDtypeStruct((channels, 4 * order), jnp.float32),
        ],
    )(keys, values, cotangent, queries, dec, weight)


def body(queries, keys, values, cotangent, residues, decays):
    n_dp = lax.axis_size("dp")
    n_ctx = lax.axis_size("ctx")
    ctx_at = lax.axis_index("ctx")
    seq_count, channels, chunk = keys.shape
    block, order = residues.shape
    length = chunk * n_ctx
    f32 = jnp.float32

    own = jnp.concatenate([residues, decays], axis=1)
    spots = n_dp * n_ctx
    params = lax.all_to_all(
        jnp.broadcast_to(own[None], (spots,) + own.shape), ("dp", "ctx"), 0, 0, tiled=True
    ).reshape(channels, 2 * order)
    dec = params[:, order:]
    scale = jnp.sqrt(1.0 - jnp.exp(-2.0 * dec / length))
    weight = params[:, :order] * scale

    pos = jnp.arange(chunk, dtype=f32)
    dk = dec[:, :, None]
    conv_intra, back_intra, stats = chunk_pass(
        keys[0], values[0], cotangent[0], queries[0], dec, weight, length
    )
    lead_fwd = jnp.exp(-dk * ((pos + 1) / length))
    lead_bwd = jnp.exp(-dk * ((chunk - pos) / length))

    stats = lax.all_to_all(
        stats.reshape(spots, block, 4 * order), ("dp", "ctx"), 0, 0, tiled=True
    ).reshape(n_dp, n_ctx, block, 4 * order)
    s_fwd = stats[..., :order]
    s_bwd = stats[..., order : 2 * order]
    c_intra = stats[..., 2 * order : 3 * order]
    c_lead = stats[..., 3 * order :]
    dec_grp = decays[None, None]
    hop_decay = dec_grp * (chunk / length)

    def exclusive_scan(state, sign):
        pad = jnp.zeros_like(state[:, :1])
        if sign > 0:
            carry = jnp.concatenate([pad, state[:, :-1]], axis=1)
        else:
            carry = jnp.concatenate([state[:, 1:], pad], axis=1)
        hop = 1
        while hop < n_ctx:
            fill = jnp.zeros_like(carry[:, :hop])
            if sign > 0:
                moved = jnp.concatenate([fill, carry[:, :-hop]], axis=1)
            else:
                moved = jnp.concatenate([carry[:, hop:], fill], axis=1)
            carry = carry + jnp.exp(-hop_decay * hop) * moved
            hop *= 2
        return carry

    carry_fwd = exclusive_scan(s_fwd, 1)
    carry_bwd = exclusive_scan(s_bwd, -1)
    total = jnp.sum(c_intra + carry_fwd * c_lead, axis=(0, 1))
    carries = lax.all_to_all(
        jnp.concatenate([carry_fwd, carry_bwd], axis=-1).reshape(spots, block, 2 * order),
        ("dp", "ctx"),
        0,
        0,
        tiled=True,
    ).reshape(channels, 2 * order)
    carry_fwd = carries[:, :order]
    carry_bwd = carries[:, order:]

    own_scale = jnp.sqrt(1.0 - jnp.exp(-2.0 * decays / length))
    grad_residues = total * own_scale / math.sqrt(seq_count * n_dp * length)

    conv_full = conv_intra + jnp.sum((weight * carry_fwd)[:, :, None] * lead_fwd, axis=1)
    back_full = back_intra + jnp.sum((weight * carry_bwd)[:, :, None] * lead_bwd, axis=1)
    conv_f = conv_full.astype(jnp.bfloat16).astype(f32)[None]
    back_f = back_full.astype(jnp.bfloat16).astype(f32)[None]
    mixed = (queries.astype(f32) * conv_f).astype(jnp.bfloat16)
    grad_queries = (cotangent.astype(f32) * conv_f).astype(jnp.bfloat16)
    grad_keys = (back_f * values.astype(f32)).astype(jnp.bfloat16)
    grad_values = (back_f * keys.astype(f32)).astype(jnp.bfloat16)
    return (mixed, grad_queries, grad_keys, grad_values, grad_residues)


def solution(mesh):
    return jax.shard_map(
        body,
        mesh=mesh,
        in_specs=(
            P("dp", None, "ctx"),
            P("dp", None, "ctx"),
            P("dp", None, "ctx"),
            P("dp", None, "ctx"),
            P(("dp", "ctx"), None),
            P(("dp", "ctx"), None),
        ),
        out_specs=(
            P("dp", None, "ctx"),
            P("dp", None, "ctx"),
            P("dp", None, "ctx"),
            P("dp", None, "ctx"),
            P(("dp", "ctx"), None),
        ),
        check_vma=False,
    )
```

```python
import functools
import math

import jax
import jax.numpy as jnp
from jax import lax
from jax.experimental import pallas as pl
from jax.sharding import PartitionSpec as P

exact_mode = lax.Precision.HIGHEST


def split_dot(x, tri):
    hi = x.astype(jnp.bfloat16)
    lo = (x - hi.astype(jnp.float32)).astype(jnp.bfloat16)
    return jnp.dot(hi, tri, preferred_element_type=jnp.float32) + jnp.dot(
        lo, tri, preferred_element_type=jnp.float32
    )


def chunk_kernel(k_ref, v_ref, c_ref, q_ref, dec_ref, w_ref, conv_ref, back_ref, stats_ref, *, length):
    f32 = jnp.float32
    rows, chunk = k_ref.shape
    order = dec_ref.shape[1]
    mid = chunk // 2
    g = (k_ref[...].astype(f32) * v_ref[...].astype(f32)).astype(jnp.bfloat16).astype(f32)
    gg = (c_ref[...].astype(f32) * q_ref[...].astype(f32)).astype(jnp.bfloat16).astype(f32)
    dec = dec_ref[...]
    w = w_ref[...]
    pos = lax.broadcasted_iota(jnp.int32, (1, chunk), 1).astype(f32)
    row_at = lax.broadcasted_iota(jnp.int32, (chunk, chunk), 0)
    col_at = lax.broadcasted_iota(jnp.int32, (chunk, chunk), 1)
    upper = (row_at <= col_at).astype(jnp.bfloat16)
    lower = (row_at >= col_at).astype(jnp.bfloat16)
    offset = (pos - mid) / length
    lane_at = lax.broadcasted_iota(jnp.int32, (8, 4 * chunk), 1)
    kind_at = lax.broadcasted_iota(jnp.int32, (8, 4 * chunk), 0)
    part_at = lane_at // chunk
    pick = (
        ((kind_at == 0) & (lane_at == chunk - 1))
        | ((kind_at == 1) & (lane_at == chunk))
        | ((kind_at == 2) & (part_at == 2))
        | ((kind_at == 3) & (part_at == 3))
    ).astype(jnp.bfloat16)
    rows_by_lanes = (((1,), (1,)), ((), ()))
    conv = jnp.zeros((rows, chunk), f32)
    back = jnp.zeros((rows, chunk), f32)
    for n in range(order):
        a = dec[:, n : n + 1]
        grow = jnp.exp(a * offset)
        shrink = jnp.exp(-a * offset)
        fwd = shrink * split_dot(g * grow, upper)
        bwd = grow * split_dot(gg * shrink, lower)
        conv = conv + w[:, n : n + 1] * fwd
        back = back + w[:, n : n + 1] * bwd
        lead = shrink * jnp.exp(-a * ((mid + 1) / length))
        joined = jnp.concatenate([fwd, bwd, gg * fwd, gg * lead], axis=1)
        hi = joined.astype(jnp.bfloat16)
        lo = (joined - hi.astype(f32)).astype(jnp.bfloat16)
        picked = lax.dot_general(
            pick, hi, rows_by_lanes, preferred_element_type=f32
        ) + lax.dot_general(pick, lo, rows_by_lanes, preferred_element_type=f32)
        stats_ref[4 * n : 4 * n + 4, :] = picked[:4]
    conv_ref[...] = conv
    back_ref[...] = back


def chunk_pass(keys, values, cotangent, queries, dec, weight, length, rows=256):
    channels, chunk = keys.shape
    order = dec.shape[1]
    rows = min(rows, channels)
    wide = pl.BlockSpec((rows, chunk), lambda i: (i, 0))
    narrow = pl.BlockSpec((rows, order), lambda i: (i, 0))
    return pl.pallas_call(
        functools.partial(chunk_kernel, length=length),
        grid=(channels // rows,),
        in_specs=[wide, wide, wide, wide, narrow, narrow],
        out_specs=[wide, wide, pl.BlockSpec((4 * order, rows), lambda i: (0, i))],
        out_shape=[
            jax.ShapeDtypeStruct((channels, chunk), jnp.float32),
            jax.ShapeDtypeStruct((channels, chunk), jnp.float32),
            jax.ShapeDtypeStruct((4 * order, channels), jnp.float32),
        ],
    )(keys, values, cotangent, queries, dec, weight)


def body(queries, keys, values, cotangent, residues, decays):
    n_dp = lax.axis_size("dp")
    n_ctx = lax.axis_size("ctx")
    ctx_at = lax.axis_index("ctx")
    seq_count, channels, chunk = keys.shape
    block, order = residues.shape
    length = chunk * n_ctx
    f32 = jnp.float32

    own = jnp.concatenate([residues, decays], axis=1)
    part = lax.all_to_all(
        jnp.broadcast_to(own[None], (n_dp,) + own.shape), "dp", 0, 0, tiled=True
    ).reshape(n_dp, 1, block, 2 * order)
    params = lax.all_to_all(
        jnp.broadcast_to(part, (n_dp, n_ctx, block, 2 * order)), "ctx", 1, 1, tiled=True
    ).reshape(channels, 2 * order)
    dec = params[:, order:]
    scale = jnp.sqrt(1.0 - jnp.exp(-2.0 * dec / length))
    weight = params[:, :order] * scale

    pos = jnp.arange(chunk, dtype=f32)
    dk = dec[:, :, None]
    conv_intra, back_intra, stats = chunk_pass(
        keys[0], values[0], cotangent[0], queries[0], dec, weight, length
    )
    stats = stats.reshape(order, 4, channels).transpose(2, 1, 0).reshape(channels, 4 * order)
    lead_fwd = jnp.exp(-dk * ((pos + 1) / length))
    lead_bwd = jnp.exp(-dk * ((chunk - pos) / length))

    groups = channels // (n_dp * n_ctx)
    stats = stats.reshape(n_dp, n_ctx, groups, 4 * order)
    stats = lax.all_to_all(stats, "ctx", 1, 1, tiled=True)
    s_fwd = stats[..., :order]
    s_bwd = stats[..., order : 2 * order]
    c_intra = stats[..., 2 * order : 3 * order]
    c_lead = stats[..., 3 * order :]
    dec_grp = lax.dynamic_slice_in_dim(
        dec.reshape(n_dp, n_ctx, groups, order), ctx_at, 1, axis=1
    )
    hop_decay = dec_grp * (chunk / length)

    def exclusive_scan(state, sign):
        pad = jnp.zeros_like(state[:, :1])
        if sign > 0:
            carry = jnp.concatenate([pad, state[:, :-1]], axis=1)
        else:
            carry = jnp.concatenate([state[:, 1:], pad], axis=1)
        hop = 1
        while hop < n_ctx:
            fill = jnp.zeros_like(carry[:, :hop])
            if sign > 0:
                moved = jnp.concatenate([fill, carry[:, :-hop]], axis=1)
            else:
                moved = jnp.concatenate([carry[:, hop:], fill], axis=1)
            carry = carry + jnp.exp(-hop_decay * hop) * moved
            hop *= 2
        return carry

    carry_fwd = exclusive_scan(s_fwd, 1)
    carry_bwd = exclusive_scan(s_bwd, -1)
    cross_grp = jnp.sum(c_intra + carry_fwd * c_lead, axis=1)
    carries = lax.all_to_all(
        jnp.concatenate([carry_fwd, carry_bwd], axis=-1), "ctx", 1, 1, tiled=True
    ).reshape(channels, 2 * order)
    carry_fwd = carries[:, :order]
    carry_bwd = carries[:, order:]
    total = jnp.sum(lax.all_to_all(cross_grp, "dp", 0, 0, tiled=True), axis=0)

    own_scale = jnp.sqrt(1.0 - jnp.exp(-2.0 * decays / length))
    grad_residues = total * own_scale / math.sqrt(seq_count * n_dp * length)

    conv_full = conv_intra + jnp.sum((weight * carry_fwd)[:, :, None] * lead_fwd, axis=1)
    back_full = back_intra + jnp.sum((weight * carry_bwd)[:, :, None] * lead_bwd, axis=1)
    conv_f = conv_full.astype(jnp.bfloat16).astype(f32)[None]
    back_f = back_full.astype(jnp.bfloat16).astype(f32)[None]
    mixed = (queries.astype(f32) * conv_f).astype(jnp.bfloat16)
    grad_queries = (cotangent.astype(f32) * conv_f).astype(jnp.bfloat16)
    grad_keys = (back_f * values.astype(f32)).astype(jnp.bfloat16)
    grad_values = (back_f * keys.astype(f32)).astype(jnp.bfloat16)
    return (mixed, grad_queries, grad_keys, grad_values, grad_residues)


def solution(mesh):
    return jax.shard_map(
        body,
        mesh=mesh,
        in_specs=(
            P("dp", None, "ctx"),
            P("dp", None, "ctx"),
            P("dp", None, "ctx"),
            P("dp", None, "ctx"),
            P(("dp", "ctx"), None),
            P(("dp", "ctx"), None),
        ),
        out_specs=(
            P("dp", None, "ctx"),
            P("dp", None, "ctx"),
            P("dp", None, "ctx"),
            P("dp", None, "ctx"),
            P(("dp", "ctx"), None),
        ),
        check_vma=False,
    )
```

```python
import functools
import math

import jax
import jax.numpy as jnp
from jax import lax
from jax.experimental import pallas as pl
from jax.sharding import PartitionSpec as P

exact_mode = lax.Precision.HIGHEST


def split_dot(x, tri):
    hi = x.astype(jnp.bfloat16)
    lo = (x - hi.astype(jnp.float32)).astype(jnp.bfloat16)
    return jnp.dot(hi, tri, preferred_element_type=jnp.float32) + jnp.dot(
        lo, tri, preferred_element_type=jnp.float32
    )


def chunk_kernel(k_ref, v_ref, c_ref, q_ref, dec_ref, w_ref, conv_ref, back_ref, stats_ref, *, length):
    f32 = jnp.float32
    rows, chunk = k_ref.shape
    order = dec_ref.shape[1]
    mid = chunk // 2
    g = (k_ref[...].astype(f32) * v_ref[...].astype(f32)).astype(jnp.bfloat16).astype(f32)
    gg = (c_ref[...].astype(f32) * q_ref[...].astype(f32)).astype(jnp.bfloat16).astype(f32)
    dec = dec_ref[...]
    w = w_ref[...]
    pos = lax.broadcasted_iota(jnp.int32, (1, chunk), 1).astype(f32)
    row_at = lax.broadcasted_iota(jnp.int32, (chunk, chunk), 0)
    col_at = lax.broadcasted_iota(jnp.int32, (chunk, chunk), 1)
    upper = (row_at <= col_at).astype(jnp.bfloat16)
    lower = (row_at >= col_at).astype(jnp.bfloat16)
    offset = (pos - mid) / length
    lane_at = lax.broadcasted_iota(jnp.int32, (8, 4 * chunk), 1)
    kind_at = lax.broadcasted_iota(jnp.int32, (8, 4 * chunk), 0)
    part_at = lane_at // chunk
    pick = (
        ((kind_at == 0) & (lane_at == chunk - 1))
        | ((kind_at == 1) & (lane_at == chunk))
        | ((kind_at == 2) & (part_at == 2))
        | ((kind_at == 3) & (part_at == 3))
    ).astype(jnp.bfloat16)
    rows_by_lanes = (((1,), (1,)), ((), ()))
    conv = jnp.zeros((rows, chunk), f32)
    back = jnp.zeros((rows, chunk), f32)
    for n in range(order):
        a = dec[:, n : n + 1]
        grow = jnp.exp(a * offset)
        shrink = jnp.exp(-a * offset)
        fwd = shrink * split_dot(g * grow, upper)
        bwd = grow * split_dot(gg * shrink, lower)
        conv = conv + w[:, n : n + 1] * fwd
        back = back + w[:, n : n + 1] * bwd
        lead = shrink * jnp.exp(-a * ((mid + 1) / length))
        joined = jnp.concatenate([fwd, bwd, gg * fwd, gg * lead], axis=1)
        hi = joined.astype(jnp.bfloat16)
        lo = (joined - hi.astype(f32)).astype(jnp.bfloat16)
        picked = lax.dot_general(
            pick, hi, rows_by_lanes, preferred_element_type=f32
        ) + lax.dot_general(pick, lo, rows_by_lanes, preferred_element_type=f32)
        stats_ref[4 * n : 4 * n + 4, :] = picked[:4]
    conv_ref[...] = conv
    back_ref[...] = back


def chunk_pass(keys, values, cotangent, queries, dec, weight, length, rows=256):
    channels, chunk = keys.shape
    order = dec.shape[1]
    rows = min(rows, channels)
    wide = pl.BlockSpec((rows, chunk), lambda i: (i, 0))
    narrow = pl.BlockSpec((rows, order), lambda i: (i, 0))
    return pl.pallas_call(
        functools.partial(chunk_kernel, length=length),
        grid=(channels // rows,),
        in_specs=[wide, wide, wide, wide, narrow, narrow],
        out_specs=[wide, wide, pl.BlockSpec((4 * order, rows), lambda i: (0, i))],
        out_shape=[
            jax.ShapeDtypeStruct((channels, chunk), jnp.float32),
            jax.ShapeDtypeStruct((channels, chunk), jnp.float32),
            jax.ShapeDtypeStruct((4 * order, channels), jnp.float32),
        ],
    )(keys, values, cotangent, queries, dec, weight)


def body(queries, keys, values, cotangent, residues, decays):
    n_dp = lax.axis_size("dp")
    n_ctx = lax.axis_size("ctx")
    ctx_at = lax.axis_index("ctx")
    seq_count, channels, chunk = keys.shape
    block, order = residues.shape
    length = chunk * n_ctx
    f32 = jnp.float32

    own = jnp.concatenate([residues, decays], axis=1)
    part = lax.all_to_all(
        jnp.broadcast_to(own[None], (n_dp,) + own.shape), "dp", 0, 0, tiled=True
    ).reshape(n_dp, 1, block, 2 * order)
    params = lax.all_to_all(
        jnp.broadcast_to(part, (n_dp, n_ctx, block, 2 * order)), "ctx", 1, 1, tiled=True
    ).reshape(channels, 2 * order)
    dec = params[:, order:]
    scale = jnp.sqrt(1.0 - jnp.exp(-2.0 * dec / length))
    weight = params[:, :order] * scale

    pos = jnp.arange(chunk, dtype=f32)
    dk = dec[:, :, None]
    conv_intra, back_intra, stats = chunk_pass(
        keys[0], values[0], cotangent[0], queries[0], dec, weight, length
    )
    stats = stats.reshape(order, 4, channels).transpose(2, 1, 0).reshape(channels, 4 * order)
    sub = 16
    outer = jnp.arange(chunk // sub, dtype=f32) * sub
    inner = jnp.arange(sub, dtype=f32)

    groups = channels // (n_dp * n_ctx)
    stats = stats.reshape(n_dp, n_ctx, groups, 4 * order)
    stats = lax.all_to_all(stats, "ctx", 1, 1, tiled=True)
    s_fwd = stats[..., :order]
    s_bwd = stats[..., order : 2 * order]
    c_intra = stats[..., 2 * order : 3 * order]
    c_lead = stats[..., 3 * order :]
    dec_grp = lax.dynamic_slice_in_dim(
        dec.reshape(n_dp, n_ctx, groups, order), ctx_at, 1, axis=1
    )
    hop_decay = dec_grp * (chunk / length)

    def exclusive_scan(state, sign):
        pad = jnp.zeros_like(state[:, :1])
        if sign > 0:
            carry = jnp.concatenate([pad, state[:, :-1]], axis=1)
        else:
            carry = jnp.concatenate([state[:, 1:], pad], axis=1)
        hop = 1
        while hop < n_ctx:
            fill = jnp.zeros_like(carry[:, :hop])
            if sign > 0:
                moved = jnp.concatenate([fill, carry[:, :-hop]], axis=1)
            else:
                moved = jnp.concatenate([carry[:, hop:], fill], axis=1)
            carry = carry + jnp.exp(-hop_decay * hop) * moved
            hop *= 2
        return carry

    carry_fwd = exclusive_scan(s_fwd, 1)
    carry_bwd = exclusive_scan(s_bwd, -1)
    cross_grp = jnp.sum(c_intra + carry_fwd * c_lead, axis=1)
    carries = lax.all_to_all(
        jnp.concatenate([carry_fwd, carry_bwd], axis=-1), "ctx", 1, 1, tiled=True
    ).reshape(channels, 2 * order)
    carry_fwd = carries[:, :order]
    carry_bwd = carries[:, order:]
    total = jnp.sum(lax.all_to_all(cross_grp, "dp", 0, 0, tiled=True), axis=0)

    own_scale = jnp.sqrt(1.0 - jnp.exp(-2.0 * decays / length))
    grad_residues = total * own_scale / math.sqrt(seq_count * n_dp * length)

    fwd_outer = (weight * carry_fwd)[:, :, None] * jnp.exp(-dk * (outer / length))
    fwd_inner = jnp.exp(-dk * ((inner + 1) / length))
    bwd_outer = (weight * carry_bwd)[:, :, None] * jnp.exp(-dk * ((chunk - outer) / length))
    bwd_inner = jnp.exp(dk * (inner / length))
    conv_carry = jnp.sum(fwd_outer[:, :, :, None] * fwd_inner[:, :, None, :], axis=1)
    back_carry = jnp.sum(bwd_outer[:, :, :, None] * bwd_inner[:, :, None, :], axis=1)
    conv_full = conv_intra + conv_carry.reshape(channels, chunk)
    back_full = back_intra + back_carry.reshape(channels, chunk)
    conv_f = conv_full.astype(jnp.bfloat16).astype(f32)[None]
    back_f = back_full.astype(jnp.bfloat16).astype(f32)[None]
    mixed = (queries.astype(f32) * conv_f).astype(jnp.bfloat16)
    grad_queries = (cotangent.astype(f32) * conv_f).astype(jnp.bfloat16)
    grad_keys = (back_f * values.astype(f32)).astype(jnp.bfloat16)
    grad_values = (back_f * keys.astype(f32)).astype(jnp.bfloat16)
    return (mixed, grad_queries, grad_keys, grad_values, grad_residues)


def solution(mesh):
    return jax.shard_map(
        body,
        mesh=mesh,
        in_specs=(
            P("dp", None, "ctx"),
            P("dp", None, "ctx"),
            P("dp", None, "ctx"),
            P("dp", None, "ctx"),
            P(("dp", "ctx"), None),
            P(("dp", "ctx"), None),
        ),
        out_specs=(
            P("dp", None, "ctx"),
            P("dp", None, "ctx"),
            P("dp", None, "ctx"),
            P("dp", None, "ctx"),
            P(("dp", "ctx"), None),
        ),
        check_vma=False,
    )
```

```python
import functools
import math

import jax
import jax.numpy as jnp
from jax import lax
from jax.experimental import pallas as pl
from jax.sharding import PartitionSpec as P

exact_mode = lax.Precision.HIGHEST


def split_dot(x, tri):
    hi = x.astype(jnp.bfloat16)
    lo = (x - hi.astype(jnp.float32)).astype(jnp.bfloat16)
    return jnp.dot(hi, tri, preferred_element_type=jnp.float32) + jnp.dot(
        lo, tri, preferred_element_type=jnp.float32
    )


def chunk_kernel(k_ref, v_ref, c_ref, q_ref, dec_ref, w_ref, conv_ref, back_ref, stats_ref, *, length):
    f32 = jnp.float32
    rows, chunk = k_ref.shape
    order = dec_ref.shape[1]
    mid = chunk // 2
    g = (k_ref[...].astype(f32) * v_ref[...].astype(f32)).astype(jnp.bfloat16).astype(f32)
    gg = (c_ref[...].astype(f32) * q_ref[...].astype(f32)).astype(jnp.bfloat16).astype(f32)
    dec = dec_ref[...]
    w = w_ref[...]
    pos = lax.broadcasted_iota(jnp.int32, (1, chunk), 1).astype(f32)
    row_at = lax.broadcasted_iota(jnp.int32, (chunk, chunk), 0)
    col_at = lax.broadcasted_iota(jnp.int32, (chunk, chunk), 1)
    upper = (row_at <= col_at).astype(jnp.bfloat16)
    lower = (row_at >= col_at).astype(jnp.bfloat16)
    offset = (pos - mid) / length
    lane_at = lax.broadcasted_iota(jnp.int32, (8, 4 * chunk), 1)
    kind_at = lax.broadcasted_iota(jnp.int32, (8, 4 * chunk), 0)
    part_at = lane_at // chunk
    pick = (
        ((kind_at == 0) & (lane_at == chunk - 1))
        | ((kind_at == 1) & (lane_at == chunk))
        | ((kind_at == 2) & (part_at == 2))
        | ((kind_at == 3) & (part_at == 3))
    ).astype(jnp.bfloat16)
    rows_by_lanes = (((1,), (1,)), ((), ()))
    conv = jnp.zeros((rows, chunk), f32)
    back = jnp.zeros((rows, chunk), f32)
    for n in range(order):
        a = dec[:, n : n + 1]
        grow = jnp.exp(a * offset)
        shrink = jnp.exp(-a * offset)
        fwd = shrink * split_dot(g * grow, upper)
        bwd = grow * split_dot(gg * shrink, lower)
        conv = conv + w[:, n : n + 1] * fwd
        back = back + w[:, n : n + 1] * bwd
        lead = shrink * jnp.exp(-a * ((mid + 1) / length))
        joined = jnp.concatenate([fwd, bwd, gg * fwd, gg * lead], axis=1)
        hi = joined.astype(jnp.bfloat16)
        lo = (joined - hi.astype(f32)).astype(jnp.bfloat16)
        picked = lax.dot_general(
            pick, hi, rows_by_lanes, preferred_element_type=f32
        ) + lax.dot_general(pick, lo, rows_by_lanes, preferred_element_type=f32)
        stats_ref[4 * n : 4 * n + 4, :] = picked[:4]
    conv_ref[...] = conv
    back_ref[...] = back


def chunk_pass(keys, values, cotangent, queries, dec, weight, length, rows=256):
    channels, chunk = keys.shape
    order = dec.shape[1]
    rows = min(rows, channels)
    wide = pl.BlockSpec((rows, chunk), lambda i: (i, 0))
    narrow = pl.BlockSpec((rows, order), lambda i: (i, 0))
    return pl.pallas_call(
        functools.partial(chunk_kernel, length=length),
        grid=(channels // rows,),
        in_specs=[wide, wide, wide, wide, narrow, narrow],
        out_specs=[wide, wide, pl.BlockSpec((4 * order, rows), lambda i: (0, i))],
        out_shape=[
            jax.ShapeDtypeStruct((channels, chunk), jnp.float32),
            jax.ShapeDtypeStruct((channels, chunk), jnp.float32),
            jax.ShapeDtypeStruct((4 * order, channels), jnp.float32),
        ],
    )(keys, values, cotangent, queries, dec, weight)


def body(queries, keys, values, cotangent, residues, decays):
    n_dp = lax.axis_size("dp")
    n_ctx = lax.axis_size("ctx")
    ctx_at = lax.axis_index("ctx")
    seq_count, channels, chunk = keys.shape
    block, order = residues.shape
    length = chunk * n_ctx
    f32 = jnp.float32

    own = jnp.concatenate([residues, decays], axis=1)
    part = lax.all_to_all(
        jnp.broadcast_to(own[None], (n_dp,) + own.shape), "dp", 0, 0, tiled=True
    ).reshape(n_dp, 1, block, 2 * order)
    params = lax.all_to_all(
        jnp.broadcast_to(part, (n_dp, n_ctx, block, 2 * order)), "ctx", 1, 1, tiled=True
    ).reshape(channels, 2 * order)
    dec = params[:, order:]
    scale = jnp.sqrt(1.0 - jnp.exp(-2.0 * dec / length))
    weight = params[:, :order] * scale

    pos = jnp.arange(chunk, dtype=f32)
    dk = dec[:, :, None]
    conv_intra, back_intra, stats = chunk_pass(
        keys[0], values[0], cotangent[0], queries[0], dec, weight, length
    )
    lead_fwd = jnp.exp(-dk * ((pos + 1) / length))
    lead_bwd = jnp.exp(-dk * ((chunk - pos) / length))

    groups = channels // (n_dp * n_ctx)
    stats = lax.all_to_all(
        stats.reshape(order, 4, n_dp, n_ctx, groups), "ctx", 3, 3, tiled=True
    )
    s_fwd = stats[:, 0]
    s_bwd = stats[:, 1]
    c_intra = stats[:, 2]
    c_lead = stats[:, 3]
    dec_grp = lax.dynamic_slice_in_dim(
        dec.reshape(n_dp, n_ctx, groups, order), ctx_at, 1, axis=1
    ).transpose(3, 0, 1, 2)
    hop_decay = dec_grp * (chunk / length)

    def exclusive_scan(state, sign):
        pad = jnp.zeros_like(state[:, :, :1])
        if sign > 0:
            carry = jnp.concatenate([pad, state[:, :, :-1]], axis=2)
        else:
            carry = jnp.concatenate([state[:, :, 1:], pad], axis=2)
        hop = 1
        while hop < n_ctx:
            fill = jnp.zeros_like(carry[:, :, :hop])
            if sign > 0:
                moved = jnp.concatenate([fill, carry[:, :, :-hop]], axis=2)
            else:
                moved = jnp.concatenate([carry[:, :, hop:], fill], axis=2)
            carry = carry + jnp.exp(-hop_decay * hop) * moved
            hop *= 2
        return carry

    carry_fwd = exclusive_scan(s_fwd, 1)
    carry_bwd = exclusive_scan(s_bwd, -1)
    cross_grp = jnp.sum(c_intra + carry_fwd * c_lead, axis=2).transpose(1, 2, 0)
    carries = lax.all_to_all(
        jnp.concatenate([carry_fwd, carry_bwd], axis=0), "ctx", 2, 2, tiled=True
    ).reshape(2 * order, channels)
    carry_fwd = carries[:order].T
    carry_bwd = carries[order:].T
    total = jnp.sum(lax.all_to_all(cross_grp, "dp", 0, 0, tiled=True), axis=0)

    own_scale = jnp.sqrt(1.0 - jnp.exp(-2.0 * decays / length))
    grad_residues = total * own_scale / math.sqrt(seq_count * n_dp * length)

    conv_full = conv_intra + jnp.sum((weight * carry_fwd)[:, :, None] * lead_fwd, axis=1)
    back_full = back_intra + jnp.sum((weight * carry_bwd)[:, :, None] * lead_bwd, axis=1)
    conv_f = conv_full.astype(jnp.bfloat16).astype(f32)[None]
    back_f = back_full.astype(jnp.bfloat16).astype(f32)[None]
    mixed = (queries.astype(f32) * conv_f).astype(jnp.bfloat16)
    grad_queries = (cotangent.astype(f32) * conv_f).astype(jnp.bfloat16)
    grad_keys = (back_f * values.astype(f32)).astype(jnp.bfloat16)
    grad_values = (back_f * keys.astype(f32)).astype(jnp.bfloat16)
    return (mixed, grad_queries, grad_keys, grad_values, grad_residues)


def solution(mesh):
    return jax.shard_map(
        body,
        mesh=mesh,
        in_specs=(
            P("dp", None, "ctx"),
            P("dp", None, "ctx"),
            P("dp", None, "ctx"),
            P("dp", None, "ctx"),
            P(("dp", "ctx"), None),
            P(("dp", "ctx"), None),
        ),
        out_specs=(
            P("dp", None, "ctx"),
            P("dp", None, "ctx"),
            P("dp", None, "ctx"),
            P("dp", None, "ctx"),
            P(("dp", "ctx"), None),
        ),
        check_vma=False,
    )
```

```python
import functools
import math

import jax
import jax.numpy as jnp
from jax import lax
from jax.experimental import pallas as pl
from jax.sharding import PartitionSpec as P

exact_mode = lax.Precision.HIGHEST


def split_dot(x, tri):
    hi = x.astype(jnp.bfloat16)
    lo = (x - hi.astype(jnp.float32)).astype(jnp.bfloat16)
    return jnp.dot(hi, tri, preferred_element_type=jnp.float32) + jnp.dot(
        lo, tri, preferred_element_type=jnp.float32
    )


def chunk_kernel(k_ref, v_ref, c_ref, q_ref, dec_ref, w_ref, conv_ref, back_ref, stats_ref, *, length):
    f32 = jnp.float32
    rows, chunk = k_ref.shape
    order = dec_ref.shape[1]
    mid = chunk // 2
    g = (k_ref[...].astype(f32) * v_ref[...].astype(f32)).astype(jnp.bfloat16).astype(f32)
    gg = (c_ref[...].astype(f32) * q_ref[...].astype(f32)).astype(jnp.bfloat16).astype(f32)
    dec = dec_ref[...]
    w = w_ref[...]
    pos = lax.broadcasted_iota(jnp.int32, (1, chunk), 1).astype(f32)
    row_at = lax.broadcasted_iota(jnp.int32, (chunk, chunk), 0)
    col_at = lax.broadcasted_iota(jnp.int32, (chunk, chunk), 1)
    upper = (row_at <= col_at).astype(jnp.bfloat16)
    lower = (row_at >= col_at).astype(jnp.bfloat16)
    offset = (pos - mid) / length
    lane_at = lax.broadcasted_iota(jnp.int32, (8, 4 * chunk), 1)
    kind_at = lax.broadcasted_iota(jnp.int32, (8, 4 * chunk), 0)
    part_at = lane_at // chunk
    pick = (
        ((kind_at == 0) & (lane_at == chunk - 1))
        | ((kind_at == 1) & (lane_at == chunk))
        | ((kind_at == 2) & (part_at == 2))
        | ((kind_at == 3) & (part_at == 3))
    ).astype(jnp.bfloat16)
    rows_by_lanes = (((1,), (1,)), ((), ()))
    conv = jnp.zeros((rows, chunk), f32)
    back = jnp.zeros((rows, chunk), f32)
    for n in range(order):
        a = dec[:, n : n + 1]
        grow = jnp.exp(a * offset)
        shrink = jnp.exp(-a * offset)
        fwd = shrink * split_dot(g * grow, upper)
        bwd = grow * split_dot(gg * shrink, lower)
        conv = conv + w[:, n : n + 1] * fwd
        back = back + w[:, n : n + 1] * bwd
        lead = shrink * jnp.exp(-a * ((mid + 1) / length))
        joined = jnp.concatenate([fwd, bwd, gg * fwd, gg * lead], axis=1)
        hi = joined.astype(jnp.bfloat16)
        lo = (joined - hi.astype(f32)).astype(jnp.bfloat16)
        picked = lax.dot_general(
            pick, hi, rows_by_lanes, preferred_element_type=f32
        ) + lax.dot_general(pick, lo, rows_by_lanes, preferred_element_type=f32)
        stats_ref[4 * n : 4 * n + 4, :] = picked[:4]
    conv_ref[...] = conv
    back_ref[...] = back


def chunk_pass(keys, values, cotangent, queries, dec, weight, length, rows=128):
    channels, chunk = keys.shape
    order = dec.shape[1]
    rows = min(rows, channels)
    wide = pl.BlockSpec((rows, chunk), lambda i: (i, 0))
    narrow = pl.BlockSpec((rows, order), lambda i: (i, 0))
    return pl.pallas_call(
        functools.partial(chunk_kernel, length=length),
        grid=(channels // rows,),
        in_specs=[wide, wide, wide, wide, narrow, narrow],
        out_specs=[wide, wide, pl.BlockSpec((4 * order, rows), lambda i: (0, i))],
        out_shape=[
            jax.ShapeDtypeStruct((channels, chunk), jnp.float32),
            jax.ShapeDtypeStruct((channels, chunk), jnp.float32),
            jax.ShapeDtypeStruct((4 * order, channels), jnp.float32),
        ],
    )(keys, values, cotangent, queries, dec, weight)


def body(queries, keys, values, cotangent, residues, decays):
    n_dp = lax.axis_size("dp")
    n_ctx = lax.axis_size("ctx")
    ctx_at = lax.axis_index("ctx")
    seq_count, channels, chunk = keys.shape
    block, order = residues.shape
    length = chunk * n_ctx
    f32 = jnp.float32

    own = jnp.concatenate([residues, decays], axis=1)
    part = lax.all_to_all(
        jnp.broadcast_to(own[None], (n_dp,) + own.shape), "dp", 0, 0, tiled=True
    ).reshape(n_dp, 1, block, 2 * order)
    params = lax.all_to_all(
        jnp.broadcast_to(part, (n_dp, n_ctx, block, 2 * order)), "ctx", 1, 1, tiled=True
    ).reshape(channels, 2 * order)
    dec = params[:, order:]
    scale = jnp.sqrt(1.0 - jnp.exp(-2.0 * dec / length))
    weight = params[:, :order] * scale

    pos = jnp.arange(chunk, dtype=f32)
    dk = dec[:, :, None]
    conv_intra, back_intra, stats = chunk_pass(
        keys[0], values[0], cotangent[0], queries[0], dec, weight, length
    )
    stats = stats.reshape(order, 4, channels).transpose(2, 1, 0).reshape(channels, 4 * order)
    lead_fwd = jnp.exp(-dk * ((pos + 1) / length))
    lead_bwd = jnp.exp(-dk * ((chunk - pos) / length))

    groups = channels // (n_dp * n_ctx)
    stats = stats.reshape(n_dp, n_ctx, groups, 4 * order)
    stats = lax.all_to_all(stats, "ctx", 1, 1, tiled=True)
    s_fwd = stats[..., :order]
    s_bwd = stats[..., order : 2 * order]
    c_intra = stats[..., 2 * order : 3 * order]
    c_lead = stats[..., 3 * order :]
    dec_grp = lax.dynamic_slice_in_dim(
        dec.reshape(n_dp, n_ctx, groups, order), ctx_at, 1, axis=1
    )
    hop_decay = dec_grp * (chunk / length)

    def exclusive_scan(state, sign):
        pad = jnp.zeros_like(state[:, :1])
        if sign > 0:
            carry = jnp.concatenate([pad, state[:, :-1]], axis=1)
        else:
            carry = jnp.concatenate([state[:, 1:], pad], axis=1)
        hop = 1
        while hop < n_ctx:
            fill = jnp.zeros_like(carry[:, :hop])
            if sign > 0:
                moved = jnp.concatenate([fill, carry[:, :-hop]], axis=1)
            else:
                moved = jnp.concatenate([carry[:, hop:], fill], axis=1)
            carry = carry + jnp.exp(-hop_decay * hop) * moved
            hop *= 2
        return carry

    carry_fwd = exclusive_scan(s_fwd, 1)
    carry_bwd = exclusive_scan(s_bwd, -1)
    cross_grp = jnp.sum(c_intra + carry_fwd * c_lead, axis=1)
    carries = lax.all_to_all(
        jnp.concatenate([carry_fwd, carry_bwd], axis=-1), "ctx", 1, 1, tiled=True
    ).reshape(channels, 2 * order)
    carry_fwd = carries[:, :order]
    carry_bwd = carries[:, order:]
    total = jnp.sum(lax.all_to_all(cross_grp, "dp", 0, 0, tiled=True), axis=0)

    own_scale = jnp.sqrt(1.0 - jnp.exp(-2.0 * decays / length))
    grad_residues = total * own_scale / math.sqrt(seq_count * n_dp * length)

    conv_full = conv_intra + jnp.sum((weight * carry_fwd)[:, :, None] * lead_fwd, axis=1)
    back_full = back_intra + jnp.sum((weight * carry_bwd)[:, :, None] * lead_bwd, axis=1)
    conv_f = conv_full.astype(jnp.bfloat16).astype(f32)[None]
    back_f = back_full.astype(jnp.bfloat16).astype(f32)[None]
    mixed = (queries.astype(f32) * conv_f).astype(jnp.bfloat16)
    grad_queries = (cotangent.astype(f32) * conv_f).astype(jnp.bfloat16)
    grad_keys = (back_f * values.astype(f32)).astype(jnp.bfloat16)
    grad_values = (back_f * keys.astype(f32)).astype(jnp.bfloat16)
    return (mixed, grad_queries, grad_keys, grad_values, grad_residues)


def solution(mesh):
    return jax.shard_map(
        body,
        mesh=mesh,
        in_specs=(
            P("dp", None, "ctx"),
            P("dp", None, "ctx"),
            P("dp", None, "ctx"),
            P("dp", None, "ctx"),
            P(("dp", "ctx"), None),
            P(("dp", "ctx"), None),
        ),
        out_specs=(
            P("dp", None, "ctx"),
            P("dp", None, "ctx"),
            P("dp", None, "ctx"),
            P("dp", None, "ctx"),
            P(("dp", "ctx"), None),
        ),
        check_vma=False,
    )
```

```python
import functools
import math

import jax
import jax.numpy as jnp
from jax import lax
from jax.experimental import pallas as pl
from jax.sharding import PartitionSpec as P

exact_mode = lax.Precision.HIGHEST


def split_dot(x, tri):
    hi = x.astype(jnp.bfloat16)
    lo = (x - hi.astype(jnp.float32)).astype(jnp.bfloat16)
    return jnp.dot(hi, tri, preferred_element_type=jnp.float32) + jnp.dot(
        lo, tri, preferred_element_type=jnp.float32
    )


def chunk_kernel(k_ref, v_ref, c_ref, q_ref, dec_ref, w_ref, conv_ref, back_ref, stats_ref, *, length):
    f32 = jnp.float32
    rows, chunk = k_ref.shape
    order = dec_ref.shape[1]
    mid = chunk // 2
    g = (k_ref[...].astype(f32) * v_ref[...].astype(f32)).astype(jnp.bfloat16).astype(f32)
    gg = (c_ref[...].astype(f32) * q_ref[...].astype(f32)).astype(jnp.bfloat16).astype(f32)
    dec = dec_ref[...]
    w = w_ref[...]
    pos = lax.broadcasted_iota(jnp.int32, (1, chunk), 1).astype(f32)
    row_at = lax.broadcasted_iota(jnp.int32, (chunk, chunk), 0)
    col_at = lax.broadcasted_iota(jnp.int32, (chunk, chunk), 1)
    upper = (row_at <= col_at).astype(jnp.bfloat16)
    lower = (row_at >= col_at).astype(jnp.bfloat16)
    offset = (pos - mid) / length
    lane_at = lax.broadcasted_iota(jnp.int32, (8, 4 * chunk), 1)
    kind_at = lax.broadcasted_iota(jnp.int32, (8, 4 * chunk), 0)
    part_at = lane_at // chunk
    pick = (
        ((kind_at == 0) & (lane_at == chunk - 1))
        | ((kind_at == 1) & (lane_at == chunk))
        | ((kind_at == 2) & (part_at == 2))
        | ((kind_at == 3) & (part_at == 3))
    ).astype(jnp.bfloat16)
    rows_by_lanes = (((1,), (1,)), ((), ()))
    conv = jnp.zeros((rows, chunk), f32)
    back = jnp.zeros((rows, chunk), f32)
    for n in range(order):
        a = dec[:, n : n + 1]
        grow = jnp.exp(a * offset)
        shrink = jnp.exp(-a * offset)
        fwd = shrink * split_dot(g * grow, upper)
        bwd = grow * split_dot(gg * shrink, lower)
        conv = conv + w[:, n : n + 1] * fwd
        back = back + w[:, n : n + 1] * bwd
        lead = shrink * jnp.exp(-a * ((mid + 1) / length))
        joined = jnp.concatenate([fwd, bwd, gg * fwd, gg * lead], axis=1)
        hi = joined.astype(jnp.bfloat16)
        lo = (joined - hi.astype(f32)).astype(jnp.bfloat16)
        picked = lax.dot_general(
            pick, hi, rows_by_lanes, preferred_element_type=f32
        ) + lax.dot_general(pick, lo, rows_by_lanes, preferred_element_type=f32)
        stats_ref[4 * n : 4 * n + 4, :] = picked[:4]
    conv_ref[...] = conv
    back_ref[...] = back


def chunk_pass(keys, values, cotangent, queries, dec, weight, length, rows=512):
    channels, chunk = keys.shape
    order = dec.shape[1]
    rows = min(rows, channels)
    wide = pl.BlockSpec((rows, chunk), lambda i: (i, 0))
    narrow = pl.BlockSpec((rows, order), lambda i: (i, 0))
    return pl.pallas_call(
        functools.partial(chunk_kernel, length=length),
        grid=(channels // rows,),
        in_specs=[wide, wide, wide, wide, narrow, narrow],
        out_specs=[wide, wide, pl.BlockSpec((4 * order, rows), lambda i: (0, i))],
        out_shape=[
            jax.ShapeDtypeStruct((channels, chunk), jnp.float32),
            jax.ShapeDtypeStruct((channels, chunk), jnp.float32),
            jax.ShapeDtypeStruct((4 * order, channels), jnp.float32),
        ],
    )(keys, values, cotangent, queries, dec, weight)


def body(queries, keys, values, cotangent, residues, decays):
    n_dp = lax.axis_size("dp")
    n_ctx = lax.axis_size("ctx")
    ctx_at = lax.axis_index("ctx")
    seq_count, channels, chunk = keys.shape
    block, order = residues.shape
    length = chunk * n_ctx
    f32 = jnp.float32

    own = jnp.concatenate([residues, decays], axis=1)
    part = lax.all_to_all(
        jnp.broadcast_to(own[None], (n_dp,) + own.shape), "dp", 0, 0, tiled=True
    ).reshape(n_dp, 1, block, 2 * order)
    params = lax.all_to_all(
        jnp.broadcast_to(part, (n_dp, n_ctx, block, 2 * order)), "ctx", 1, 1, tiled=True
    ).reshape(channels, 2 * order)
    dec = params[:, order:]
    scale = jnp.sqrt(1.0 - jnp.exp(-2.0 * dec / length))
    weight = params[:, :order] * scale

    pos = jnp.arange(chunk, dtype=f32)
    dk = dec[:, :, None]
    conv_intra, back_intra, stats = chunk_pass(
        keys[0], values[0], cotangent[0], queries[0], dec, weight, length
    )
    stats = stats.reshape(order, 4, channels).transpose(2, 1, 0).reshape(channels, 4 * order)
    lead_fwd = jnp.exp(-dk * ((pos + 1) / length))
    lead_bwd = jnp.exp(-dk * ((chunk - pos) / length))

    groups = channels // (n_dp * n_ctx)
    stats = stats.reshape(n_dp, n_ctx, groups, 4 * order)
    stats = lax.all_to_all(stats, "ctx", 1, 1, tiled=True)
    s_fwd = stats[..., :order]
    s_bwd = stats[..., order : 2 * order]
    c_intra = stats[..., 2 * order : 3 * order]
    c_lead = stats[..., 3 * order :]
    dec_grp = lax.dynamic_slice_in_dim(
        dec.reshape(n_dp, n_ctx, groups, order), ctx_at, 1, axis=1
    )
    hop_decay = dec_grp * (chunk / length)

    def exclusive_scan(state, sign):
        pad = jnp.zeros_like(state[:, :1])
        if sign > 0:
            carry = jnp.concatenate([pad, state[:, :-1]], axis=1)
        else:
            carry = jnp.concatenate([state[:, 1:], pad], axis=1)
        hop = 1
        while hop < n_ctx:
            fill = jnp.zeros_like(carry[:, :hop])
            if sign > 0:
                moved = jnp.concatenate([fill, carry[:, :-hop]], axis=1)
            else:
                moved = jnp.concatenate([carry[:, hop:], fill], axis=1)
            carry = carry + jnp.exp(-hop_decay * hop) * moved
            hop *= 2
        return carry

    carry_fwd = exclusive_scan(s_fwd, 1)
    carry_bwd = exclusive_scan(s_bwd, -1)
    cross_grp = jnp.sum(c_intra + carry_fwd * c_lead, axis=1)
    carries = lax.all_to_all(
        jnp.concatenate([carry_fwd, carry_bwd], axis=-1), "ctx", 1, 1, tiled=True
    ).reshape(channels, 2 * order)
    carry_fwd = carries[:, :order]
    carry_bwd = carries[:, order:]
    total = jnp.sum(lax.all_to_all(cross_grp, "dp", 0, 0, tiled=True), axis=0)

    own_scale = jnp.sqrt(1.0 - jnp.exp(-2.0 * decays / length))
    grad_residues = total * own_scale / math.sqrt(seq_count * n_dp * length)

    conv_full = conv_intra + jnp.sum((weight * carry_fwd)[:, :, None] * lead_fwd, axis=1)
    back_full = back_intra + jnp.sum((weight * carry_bwd)[:, :, None] * lead_bwd, axis=1)
    conv_f = conv_full.astype(jnp.bfloat16).astype(f32)[None]
    back_f = back_full.astype(jnp.bfloat16).astype(f32)[None]
    mixed = (queries.astype(f32) * conv_f).astype(jnp.bfloat16)
    grad_queries = (cotangent.astype(f32) * conv_f).astype(jnp.bfloat16)
    grad_keys = (back_f * values.astype(f32)).astype(jnp.bfloat16)
    grad_values = (back_f * keys.astype(f32)).astype(jnp.bfloat16)
    return (mixed, grad_queries, grad_keys, grad_values, grad_residues)


def solution(mesh):
    return jax.shard_map(
        body,
        mesh=mesh,
        in_specs=(
            P("dp", None, "ctx"),
            P("dp", None, "ctx"),
            P("dp", None, "ctx"),
            P("dp", None, "ctx"),
            P(("dp", "ctx"), None),
            P(("dp", "ctx"), None),
        ),
        out_specs=(
            P("dp", None, "ctx"),
            P("dp", None, "ctx"),
            P("dp", None, "ctx"),
            P("dp", None, "ctx"),
            P(("dp", "ctx"), None),
        ),
        check_vma=False,
    )
```

```python
import functools
import math

import jax
import jax.numpy as jnp
from jax import lax
from jax.experimental import pallas as pl
from jax.sharding import PartitionSpec as P

exact_mode = lax.Precision.HIGHEST


def split_dot(x, tri):
    hi = x.astype(jnp.bfloat16)
    lo = (x - hi.astype(jnp.float32)).astype(jnp.bfloat16)
    return jnp.dot(hi, tri, preferred_element_type=jnp.float32) + jnp.dot(
        lo, tri, preferred_element_type=jnp.float32
    )


def chunk_kernel(k_ref, v_ref, c_ref, q_ref, dec_ref, w_ref, conv_ref, back_ref, stats_ref, *, length):
    f32 = jnp.float32
    rows, chunk = k_ref.shape
    order = dec_ref.shape[1]
    mid = chunk // 2
    g = (k_ref[...].astype(f32) * v_ref[...].astype(f32)).astype(jnp.bfloat16).astype(f32)
    gg = (c_ref[...].astype(f32) * q_ref[...].astype(f32)).astype(jnp.bfloat16).astype(f32)
    dec = dec_ref[...]
    w = w_ref[...]
    pos = lax.broadcasted_iota(jnp.int32, (1, chunk), 1).astype(f32)
    row_at = lax.broadcasted_iota(jnp.int32, (chunk, chunk), 0)
    col_at = lax.broadcasted_iota(jnp.int32, (chunk, chunk), 1)
    upper = (row_at <= col_at).astype(jnp.bfloat16)
    lower = (row_at >= col_at).astype(jnp.bfloat16)
    offset = (pos - mid) / length
    lane_at = lax.broadcasted_iota(jnp.int32, (8, 4 * chunk), 1)
    kind_at = lax.broadcasted_iota(jnp.int32, (8, 4 * chunk), 0)
    part_at = lane_at // chunk
    pick = (
        ((kind_at == 0) & (lane_at == chunk - 1))
        | ((kind_at == 1) & (lane_at == chunk))
        | ((kind_at == 2) & (part_at == 2))
        | ((kind_at == 3) & (part_at == 3))
    ).astype(jnp.bfloat16)
    rows_by_lanes = (((1,), (1,)), ((), ()))
    conv = jnp.zeros((rows, chunk), f32)
    back = jnp.zeros((rows, chunk), f32)
    for n in range(order):
        a = dec[:, n : n + 1]
        grow = jnp.exp(a * offset)
        shrink = jnp.exp(-a * offset)
        fwd = shrink * split_dot(g * grow, upper)
        bwd = grow * split_dot(gg * shrink, lower)
        conv = conv + w[:, n : n + 1] * fwd
        back = back + w[:, n : n + 1] * bwd
        lead = shrink * jnp.exp(-a * ((mid + 1) / length))
        joined = jnp.concatenate([fwd, bwd, gg * fwd, gg * lead], axis=1)
        hi = joined.astype(jnp.bfloat16)
        lo = (joined - hi.astype(f32)).astype(jnp.bfloat16)
        picked = lax.dot_general(
            pick, hi, rows_by_lanes, preferred_element_type=f32
        ) + lax.dot_general(pick, lo, rows_by_lanes, preferred_element_type=f32)
        stats_ref[4 * n : 4 * n + 4, :] = picked[:4]
    conv_ref[...] = conv
    back_ref[...] = back


def chunk_pass(keys, values, cotangent, queries, dec, weight, length, rows=256):
    channels, chunk = keys.shape
    order = dec.shape[1]
    rows = min(rows, channels)
    wide = pl.BlockSpec((rows, chunk), lambda i: (i, 0))
    narrow = pl.BlockSpec((rows, order), lambda i: (i, 0))
    return pl.pallas_call(
        functools.partial(chunk_kernel, length=length),
        grid=(channels // rows,),
        in_specs=[wide, wide, wide, wide, narrow, narrow],
        out_specs=[wide, wide, pl.BlockSpec((4 * order, rows), lambda i: (0, i))],
        out_shape=[
            jax.ShapeDtypeStruct((channels, chunk), jnp.float32),
            jax.ShapeDtypeStruct((channels, chunk), jnp.float32),
            jax.ShapeDtypeStruct((4 * order, channels), jnp.float32),
        ],
    )(keys, values, cotangent, queries, dec, weight)


def body(queries, keys, values, cotangent, residues, decays):
    n_dp = lax.axis_size("dp")
    n_ctx = lax.axis_size("ctx")
    ctx_at = lax.axis_index("ctx")
    seq_count, channels, chunk = keys.shape
    block, order = residues.shape
    length = chunk * n_ctx
    f32 = jnp.float32

    own = jnp.concatenate([residues, decays], axis=1)
    part = lax.all_to_all(
        jnp.broadcast_to(own[None], (n_dp,) + own.shape), "dp", 0, 0, tiled=True
    ).reshape(n_dp, 1, block, 2 * order)
    params = lax.all_to_all(
        jnp.broadcast_to(part, (n_dp, n_ctx, block, 2 * order)), "ctx", 1, 1, tiled=True
    ).reshape(channels, 2 * order)
    dec = params[:, order:]
    scale = jnp.sqrt(1.0 - jnp.exp(-2.0 * dec / length))
    weight = params[:, :order] * scale

    pos = jnp.arange(chunk, dtype=f32)
    dk = dec[:, :, None]
    conv_intra, back_intra, stats = chunk_pass(
        keys[0], values[0], cotangent[0], queries[0], dec, weight, length
    )
    stats = stats.reshape(order, 4, channels).transpose(2, 1, 0).reshape(channels, 4 * order)
    lead_fwd = jnp.exp(-dk * ((pos + 1) / length))

    groups = channels // (n_dp * n_ctx)
    stats = stats.reshape(n_dp, n_ctx, groups, 4 * order)
    stats = lax.all_to_all(stats, "ctx", 1, 1, tiled=True)
    s_fwd = stats[..., :order]
    s_bwd = stats[..., order : 2 * order]
    c_intra = stats[..., 2 * order : 3 * order]
    c_lead = stats[..., 3 * order :]
    dec_grp = lax.dynamic_slice_in_dim(
        dec.reshape(n_dp, n_ctx, groups, order), ctx_at, 1, axis=1
    )
    hop_decay = dec_grp * (chunk / length)

    def exclusive_scan(state, sign):
        pad = jnp.zeros_like(state[:, :1])
        if sign > 0:
            carry = jnp.concatenate([pad, state[:, :-1]], axis=1)
        else:
            carry = jnp.concatenate([state[:, 1:], pad], axis=1)
        hop = 1
        while hop < n_ctx:
            fill = jnp.zeros_like(carry[:, :hop])
            if sign > 0:
                moved = jnp.concatenate([fill, carry[:, :-hop]], axis=1)
            else:
                moved = jnp.concatenate([carry[:, hop:], fill], axis=1)
            carry = carry + jnp.exp(-hop_decay * hop) * moved
            hop *= 2
        return carry

    carry_fwd = exclusive_scan(s_fwd, 1)
    carry_bwd = exclusive_scan(s_bwd, -1)
    cross_grp = jnp.sum(c_intra + carry_fwd * c_lead, axis=1)
    carries = lax.all_to_all(
        jnp.concatenate([carry_fwd, carry_bwd], axis=-1), "ctx", 1, 1, tiled=True
    ).reshape(channels, 2 * order)
    carry_fwd = carries[:, :order]
    carry_bwd = carries[:, order:]
    total = jnp.sum(lax.all_to_all(cross_grp, "dp", 0, 0, tiled=True), axis=0)

    own_scale = jnp.sqrt(1.0 - jnp.exp(-2.0 * decays / length))
    grad_residues = total * own_scale / math.sqrt(seq_count * n_dp * length)

    conv_full = conv_intra + jnp.sum((weight * carry_fwd)[:, :, None] * lead_fwd, axis=1)
    back_full = back_intra + jnp.flip(
        jnp.sum((weight * carry_bwd)[:, :, None] * lead_fwd, axis=1), axis=1
    )
    conv_f = conv_full.astype(jnp.bfloat16).astype(f32)[None]
    back_f = back_full.astype(jnp.bfloat16).astype(f32)[None]
    mixed = (queries.astype(f32) * conv_f).astype(jnp.bfloat16)
    grad_queries = (cotangent.astype(f32) * conv_f).astype(jnp.bfloat16)
    grad_keys = (back_f * values.astype(f32)).astype(jnp.bfloat16)
    grad_values = (back_f * keys.astype(f32)).astype(jnp.bfloat16)
    return (mixed, grad_queries, grad_keys, grad_values, grad_residues)


def solution(mesh):
    return jax.shard_map(
        body,
        mesh=mesh,
        in_specs=(
            P("dp", None, "ctx"),
            P("dp", None, "ctx"),
            P("dp", None, "ctx"),
            P("dp", None, "ctx"),
            P(("dp", "ctx"), None),
            P(("dp", "ctx"), None),
        ),
        out_specs=(
            P("dp", None, "ctx"),
            P("dp", None, "ctx"),
            P("dp", None, "ctx"),
            P("dp", None, "ctx"),
            P(("dp", "ctx"), None),
        ),
        check_vma=False,
    )
```
